256 devices in a mesh: src: 64 (over z, y_lo, x), rcv: 4 (over y_hi, core).
Axes of the slice: x: 4, y: 4 (y_hi: 2, y_lo: 2; y = y_hi * 2 + y_lo), z: 8, core: 2. Of those that a mesh axis runs over, the one named last changes fastest.
Arguments:
- probes: bfloat16 [256, 1024, 256], P('rcv', 'src'), may hold values from -6 to 6
- kappa: float32 [1024, 256], P('src'), may hold values from 0.02 to 0.24
- footprint: bfloat16 [64, 4, 192, 128, 128], P('src', 'rcv'), may hold values from -0.0390625 to 0.0390625
- block_source: int32 [64, 4, 192], P('src', 'rcv'), may hold values from 0 to 31
- block_receptor: int32 [64, 4, 192], P('src', 'rcv'), may hold values from 0 to 15
- block_count: int32 [64, 4], P('src', 'rcv'), may hold values from 1 to 192, as said below
- obs_weight: float32 [8192], P('rcv'), may hold values from 1 to 8
Outputs:
- hessian_probe: float32 [256, 1024, 256], P('rcv', 'src')
The draws below stay inside these ranges and needn't reach their ends.
Inputs may be any that keep to these rules, and one draw needn't show every extreme that they name: Slots 0 to block_count - 1 of a tile and group hold its footprint blocks, later slots are unused; some tile and group uses all 192 slots.
All inputs are finite; a program needn't handle non-finite values.
Results may differ from the reference program's by a relative error of at most 0.006.
Values may be sent and summed in bfloat16 or wider, within the bound.
A program may use at most 64 MiB of HBM per device.

```python
import math
import jax
import jax.numpy as jnp
from jax import lax

BLK = 128
NLON = 256
RB_LOC = 16
NB = 192
SMOOTH = 4
SB = 32
NLAT = 1024
P_SIZE = 256
NREC = 8192
N_SRC = 64
N_RCV = 4


def draw_block_count(key, part):
    first_key, second_key, third_key = jax.random.split(key, 3)
    factor_one = jax.random.randint(first_key, (N_SRC, N_RCV), 0, NB)
    factor_two = jax.random.randint(second_key, (N_SRC, N_RCV), 0, NB)
    counts = factor_one * factor_two // NB + 1
    busiest = jax.random.randint(third_key, (), 0, N_SRC * N_RCV)
    flat_counts = jnp.where(jnp.arange(N_SRC * N_RCV) == busiest, NB, counts.reshape(-1))
    return flat_counts.reshape(N_SRC, N_RCV).astype(jnp.int32)


def touch_ends(drawn, own_key, smallest, largest):
    index_at = [jax.random.randint(jax.random.fold_in(own_key, axis), (), 0, length) for axis, length in enumerate(drawn.shape)]
    longest = drawn.shape.index(max(drawn.shape))
    neighbour = index_at[:longest] + [(index_at[longest] + 1) % drawn.shape[longest]] + index_at[longest + 1:]
    return drawn.at[tuple(index_at)].set(smallest).at[tuple(neighbour)].set(largest)


def shard_levels(rng, shape, shards, low, high):
    level, own = 1.0, jax.random.fold_in(rng, 6)
    for position, blocks in shards:
        heights = jnp.exp(jax.random.uniform(jax.random.fold_in(own, position), (blocks,), jnp.float32, low / len(shards), high / len(shards)))
        level = level * jnp.repeat(heights, shape[position] // blocks).reshape([-1 if axis == position else 1 for axis in range(len(shape))])
    return level


def centred(key, shape, spread, limit, cuts=(), kind=jnp.bfloat16):
    gain = shard_levels(key, shape, cuts, -0.22, 0.18) if cuts else 1.0
    entries = jax.random.normal(key, shape, jnp.float32) * spread * gain
    return jnp.minimum(jnp.maximum(entries, -limit), limit).astype(kind)


def setup_inputs(seed: int = 0) -> dict:
    key_list = jax.random.split(jax.random.key(seed), 8)
    probes = centred(key_list[0], (P_SIZE, NLAT, NLON), 1.0, 6.0, ((0, 4), (1, 64)))
    kappa = jnp.clip(jnp.exp(math.log(0.24) - 2.4849066 * jax.random.uniform(key_list[1], (NLAT, NLON), jnp.float32) ** shard_levels(key_list[1], (NLAT, NLON), ((0, 64),), -0.2, 0.2)), 0.02, 0.24)
    footprint = centred(key_list[2], (N_SRC, N_RCV, NB, BLK, BLK), (N_SRC * NB * BLK // (4 * RB_LOC)) ** -0.5, 0.0390625, ((0, 64), (1, 4)))
    block_source = touch_ends(jax.random.randint(key_list[3], (N_SRC, N_RCV, NB), 0, SB), jax.random.fold_in(key_list[3], 1), 0, SB - 1).astype(jnp.int32)
    block_receptor = touch_ends(jax.random.randint(key_list[4], (N_SRC, N_RCV, NB), 0, RB_LOC), jax.random.fold_in(key_list[4], 1), 0, RB_LOC - 1).astype(jnp.int32)
    block_count = draw_block_count(jax.random.fold_in(key_list[7], 71), 0)
    obs_weight = jnp.clip(jnp.exp(math.log(8.0) - 2.0794415 * jax.random.uniform(key_list[6], (NREC,), jnp.float32) ** shard_levels(key_list[6], (NREC,), ((0, 4),), -0.2, 0.2)), 1.0, 8.0)
    return {"probes": probes, "kappa": kappa, "footprint": footprint, "block_source": block_source, "block_receptor": block_receptor, "block_count": block_count, "obs_weight": obs_weight}


def laplacian_operator(emission_source_field):
    padded = jnp.pad(emission_source_field, ((0, 0), (1, 1), (1, 1)))
    return padded[:, 2:, 1:-1] + padded[:, :-2, 1:-1] + padded[:, 1:-1, 2:] + padded[:, 1:-1, :-2] - 4.0 * emission_source_field


def device_forward(blocks, sources, receptors, used_slots, tile_field):
    selected_entries = jnp.take(tile_field, sources, axis=0).astype(jnp.float32)
    hessian_result = jnp.einsum("nrc,ncp->nrp", blocks.astype(jnp.float32), selected_entries)
    in_use = jnp.arange(blocks.shape[0], dtype=jnp.int32) < used_slots
    onehot = ((receptors[:, None] == jnp.arange(RB_LOC, dtype=jnp.int32)[None, :]) & in_use[:, None]).astype(jnp.float32)
    return jnp.einsum("nrp,nb->brp", hessian_result, onehot, precision=lax.Precision.HIGHEST)


def device_adjoint(blocks, sources, receptors, used_slots, weighted_group):
    selected_entries = jnp.take(weighted_group, receptors, axis=0).astype(jnp.float32)
    hessian_result = jnp.einsum("nrc,nrp->ncp", blocks.astype(jnp.float32), selected_entries)
    in_use = jnp.arange(blocks.shape[0], dtype=jnp.int32) < used_slots
    onehot = ((sources[:, None] == jnp.arange(SB, dtype=jnp.int32)[None, :]) & in_use[:, None]).astype(jnp.float32)
    return jnp.einsum("ncp,ns->scp", hessian_result, onehot, precision=lax.Precision.HIGHEST)


def reference(probes, kappa, footprint, block_source, block_receptor, block_count, obs_weight):
    smoothed = probes.astype(jnp.float32)
    for repeat in range(SMOOTH):
        smoothed = smoothed + kappa * laplacian_operator(smoothed)
    truncated_field = lax.optimization_barrier(smoothed.astype(jnp.bfloat16))
    tile_fields = truncated_field.reshape(P_SIZE, N_SRC, SB, BLK).transpose(1, 2, 3, 0)

    def forward_tile(running, inputs):
        blocks, sources, receptors, counts, tile_field = inputs
        block_terms = jax.vmap(device_forward, in_axes=(0, 0, 0, 0, None))(blocks, sources, receptors, counts, tile_field)
        return running + block_terms, None

    initial = jnp.zeros((N_RCV, RB_LOC, BLK, P_SIZE), jnp.float32)
    evolved, unused = lax.scan(forward_tile, initial, (footprint, block_source, block_receptor, block_count, tile_fields))
    weighted = lax.optimization_barrier((obs_weight.reshape(N_RCV, RB_LOC, BLK, 1) * evolved).astype(jnp.bfloat16))

    def adjoint_tile(running, inputs):
        blocks, sources, receptors, counts = inputs
        block_terms = jax.vmap(device_adjoint)(blocks, sources, receptors, counts, weighted)
        rounded = lax.optimization_barrier(block_terms.astype(jnp.bfloat16))
        return running, jnp.sum(rounded.astype(jnp.float32), axis=0)

    dummy = jnp.zeros((), jnp.float32)
    dummy, adjoint_pass = lax.scan(adjoint_tile, dummy, (footprint, block_source, block_receptor, block_count))
    adjoint_pass = adjoint_pass.transpose(3, 0, 1, 2).reshape(P_SIZE, NLAT, NLON)
    back = adjoint_pass
    for repeat in range(SMOOTH):
        back = back + laplacian_operator(kappa * back)
    return probes.astype(jnp.float32) + back
```

```python
import jax
import jax.numpy as jnp
from jax import lax
from jax.experimental import pallas as pl
from jax.experimental.pallas import tpu as pltpu
from jax.sharding import PartitionSpec as P

BLK = 128
RB = 16
SB = 32
NB = 192
LAT = 16
LON = 256
PROBES = 64
GROUPS = 4
GP = PROBES // GROUPS
STEPS = 4
PAD = LAT + 2 * STEPS
CHUNK = 16
NCHUNK = NB // CHUNK
N_SRC = 64
MESH = pl.DeviceIdType.MESH
F32 = jnp.float32
BF16 = jnp.bfloat16
VM = pl.BlockSpec(memory_space=pltpu.VMEM)
SM = pl.BlockSpec(memory_space=pltpu.SMEM)
ANY = pl.BlockSpec(memory_space=pl.ANY)
DMA = pltpu.SemaphoreType.DMA


def remote(src, dst, send, recv, device):
    return pltpu.make_async_remote_copy(
        src_ref=src, dst_ref=dst, send_sem=send, recv_sem=recv, device_id=device, device_id_type=MESH
    )


def meet(peers):
    barrier = pltpu.get_barrier_semaphore()
    for peer in peers:
        pl.semaphore_signal(barrier, inc=1, device_id=peer, device_id_type=MESH)
    pl.semaphore_wait(barrier, len(peers))


def ring_places():
    s = lax.axis_index("src")
    r = lax.axis_index("rcv")
    y_lo = lax.rem(s // 4, 2)
    pair = s + 4 - 8 * y_lo
    y_hi = r // 2
    core = lax.rem(r, 2)
    other = lax.rem(r + 2, 4)
    sib_r = y_hi * 2 + 1 - core
    far_sib_r = (1 - y_hi) * 2 + 1 - core
    plus = (pair, lax.rem(r + 2 * y_lo, 4))
    minus = (pair, lax.rem(r + 2 * (1 - y_lo), 4))
    north = (lax.rem(s + N_SRC - 1, N_SRC), r)
    south = (lax.rem(s + 1, N_SRC), r)
    return s, r, other, sib_r, far_sib_r, plus, minus, north, south


def onward(group, plus, minus):
    even = lax.rem(group, 2) == 0
    return (plus[0], jnp.where(even, plus[1], minus[1]))


def west_east(value, lane):
    west = jnp.where(lane == 0, 0.0, pltpu.roll(value, 1, 1))
    east = jnp.where(lane == LON - 1, 0.0, pltpu.roll(value, LON - 1, 1))
    return west + east


def smooth_gather(
    probes_ref, kappa_ref, out_ref, kext_ref,
    xl, xr, xt, kb, fa, fb, relay,
    halo_send, halo_recv, sib_send, sib_recv, out_send, out_recv, rel_send, rel_recv, fwd_send, fwd_recv,
):
    s, r, other, sib_r, far_sib_r, plus, minus, north, south = ring_places()
    sib = (s, sib_r)
    xl[...] = probes_ref[:, :BLK].astype(F32)
    xr[...] = probes_ref[:, BLK:].astype(F32)
    for l in list(range(STEPS)) + list(range(LAT - STEPS, LAT)) + list(range(STEPS, LAT - STEPS)):
        rows = pl.ds(l, PROBES, stride=LAT)
        xt[STEPS + l, :, :BLK] = xl[rows, :].astype(BF16)
        xt[STEPS + l, :, BLK:] = xr[rows, :].astype(BF16)
    kext_ref[pl.ds(8, LAT), :] = kappa_ref[...]
    meet((north, south, sib, plus, minus))
    halos = [
        remote(xt.at[pl.ds(STEPS, STEPS)], xt.at[pl.ds(STEPS + LAT, STEPS)], halo_send.at[0], halo_recv.at[0], north),
        remote(xt.at[pl.ds(LAT, STEPS)], xt.at[pl.ds(0, STEPS)], halo_send.at[1], halo_recv.at[1], south),
        remote(kappa_ref.at[pl.ds(0, 8)], kext_ref.at[pl.ds(24, 8)], halo_send.at[2], halo_recv.at[2], north),
        remote(kappa_ref.at[pl.ds(8, 8)], kext_ref.at[pl.ds(0, 8)], halo_send.at[3], halo_recv.at[3], south),
    ]
    for copy in halos:
        copy.start()
    for copy in halos:
        copy.wait()
    north_in = jnp.where(s > 0, 1.0, 0.0).astype(F32)
    south_in = jnp.where(s < N_SRC - 1, 1.0, 0.0).astype(F32)
    kext_ref[pl.ds(0, 8), :] = kext_ref[pl.ds(0, 8), :] * north_in
    kext_ref[pl.ds(24, 8), :] = kext_ref[pl.ds(24, 8), :] * south_in
    for l in range(PAD):
        kb[l] = jnp.broadcast_to(kext_ref[pl.ds(l + 4, 1), :], (GP, LON))
    lane = lax.broadcasted_iota(jnp.int32, (GP, LON), 1)

    def sibling_copy(g):
        return remote(out_ref.at[r, :, g], out_ref.at[r, :, g], sib_send.at[g], sib_recv.at[g], sib)

    def outward_copy(g):
        return remote(out_ref.at[r, :, g], relay.at[g], out_send.at[g], out_recv.at[g], onward(g, plus, minus))

    def relay_copy(g):
        even = lax.rem(g, 2) == 0
        slot = jnp.where(even, minus[1], plus[1])
        return remote(relay.at[g], out_ref.at[slot, :, g], rel_send.at[g], rel_recv.at[g], onward(g, plus, minus))

    def share_copy(g):
        return remote(out_ref.at[other, :, g], out_ref.at[other, :, g], fwd_send.at[g], fwd_recv.at[g], sib)

    def one_group(g, carry):
        rows = pl.ds(pl.multiple_of(g * GP, GP), GP)
        for l in range(PAD):
            scale = north_in if l < STEPS else south_in if l >= STEPS + LAT else None
            value = xt[l, rows, :].astype(F32)
            fa[l] = value if scale is None else value * scale
        for step in range(STEPS):
            old, new = (fa, fb) if step % 2 == 0 else (fb, fa)
            for l in range(step + 1, PAD - step - 1):
                c = old[l]
                v = c + kb[l] * (old[l - 1] + old[l + 1] + west_east(c, lane) - 4.0 * c)
                if step < STEPS - 1:
                    new[l] = v
                else:
                    j = 2 * (l - STEPS)
                    out_ref[r, j, g] = v[:, :BLK].astype(BF16)
                    out_ref[r, j + 1, g] = v[:, BLK:].astype(BF16)
        outward_copy(g).start()
        sibling_copy(g).start()
        return carry

    lax.fori_loop(0, GROUPS, one_group, 0)

    def pass_on(g, carry):
        outward_copy(g).wait_recv()
        relay_copy(g).start()
        return carry

    lax.fori_loop(0, GROUPS, pass_on, 0)

    def share(g, carry):
        relay_copy(g).wait_recv()
        share_copy(g).start()
        return carry

    lax.fori_loop(0, GROUPS, share, 0)

    def drain(g, carry):
        outward_copy(g).wait_send()
        sibling_copy(g).wait()
        relay_copy(g).wait_send()
        share_copy(g).wait()
        return carry

    lax.fori_loop(0, GROUPS, drain, 0)


def forward_blocks(src_ref, rec_ref, cnt_ref, field_ref, blocks_hbm, out_ref, acc, blocks, sems):
    copies = [
        pltpu.make_async_copy(blocks_hbm.at[pl.ds(c * CHUNK, CHUNK)], blocks.at[pl.ds(c * CHUNK, CHUNK)], sems.at[c])
        for c in range(NCHUNK)
    ]
    for copy in copies:
        copy.start()
    count = cnt_ref[0]

    def clear(b, carry):
        acc[b] = jnp.zeros((4 * PROBES, BLK), F32)
        return carry

    lax.fori_loop(0, RB + 1, clear, 0)

    def four(q, carry):
        terms = []
        for u in range(4):
            n = q * 4 + u
            lhs = field_ref[:, src_ref[n]].reshape(4 * PROBES, BLK)
            terms.append(
                lax.dot_general(lhs, blocks[n], (((1,), (1,)), ((), ())), preferred_element_type=F32)
            )
        for u in range(4):
            n = q * 4 + u
            b = jnp.where(n < count, rec_ref[n], RB)
            acc[b] = acc[b] + terms[u]
        return carry

    for c in range(NCHUNK):
        copies[c].wait()
        quads = jnp.clip((count - c * CHUNK + 3) // 4, 0, CHUNK // 4)
        lax.fori_loop(c * (CHUNK // 4), c * (CHUNK // 4) + quads, four, 0)

    def finish(b, carry):
        for q in range(4):
            out_ref[q, b] = acc[b, q * PROBES : (q + 1) * PROBES, :].astype(BF16)
        return carry

    lax.fori_loop(0, RB, finish, 0)


def adjoint_blocks(src_ref, rec_ref, cnt_ref, weighted_ref, blocks_hbm, out_ref, acc, blocks, sems):
    copies = [
        pltpu.make_async_copy(blocks_hbm.at[pl.ds(c * CHUNK, CHUNK)], blocks.at[pl.ds(c * CHUNK, CHUNK)], sems.at[c])
        for c in range(NCHUNK)
    ]
    for copy in copies:
        copy.start()
    count = cnt_ref[0]

    def clear(b, carry):
        acc[b] = jnp.zeros((4 * PROBES, BLK), F32)
        return carry

    lax.fori_loop(0, SB + 1, clear, 0)

    def four(q, carry):
        terms = []
        for u in range(4):
            n = q * 4 + u
            lhs = weighted_ref[:, rec_ref[n]].reshape(4 * PROBES, BLK)
            terms.append(
                lax.dot_general(lhs, blocks[n], (((1,), (0,)), ((), ())), preferred_element_type=F32)
            )
        for u in range(4):
            n = q * 4 + u
            b = jnp.where(n < count, src_ref[n], SB)
            acc[b] = acc[b] + terms[u]
        return carry

    for c in range(NCHUNK):
        copies[c].wait()
        quads = jnp.clip((count - c * CHUNK + 3) // 4, 0, CHUNK // 4)
        lax.fori_loop(c * (CHUNK // 4), c * (CHUNK // 4) + quads, four, 0)

    def finish(b, carry):
        for q in range(4):
            out_ref[q, b] = acc[b, q * PROBES : (q + 1) * PROBES, :].astype(BF16)
        return carry

    lax.fori_loop(0, SB, finish, 0)


HALF = RB // 2


def reduce_weight_gather(
    part_ref, weight_ref, out_ref,
    a_east, a_west, s_east, s_west, d_lo, d_hi, b_lo, b_hi, total, landed,
    x_send, x_recv, z_send, z_recv, a_send, a_recv, g_send, g_recv,
):
    s = lax.axis_index("src")
    r = lax.axis_index("rcv")
    x = lax.rem(s, 4)
    b0 = s // 4
    xe = lax.rem(x + 1, 4)
    xw = lax.rem(x + 3, 4)
    xo = lax.rem(x + 2, 4)
    east = (b0 * 4 + xe, r)
    west = (b0 * 4 + xw, r)

    def peer(k):
        return (lax.rem(b0 + k, RB) * 4 + x, r)

    barrier = pltpu.get_barrier_semaphore()
    pl.semaphore_signal(barrier, inc=1, device_id=east, device_id_type=MESH)
    pl.semaphore_signal(barrier, inc=1, device_id=west, device_id_type=MESH)

    def greet(k, carry):
        pl.semaphore_signal(barrier, inc=1, device_id=peer(k), device_id_type=MESH)
        return carry

    lax.fori_loop(1, RB, greet, 0)
    pl.semaphore_wait(barrier, RB + 1)

    lo, hi = pl.ds(0, HALF), pl.ds(HALF, HALF)
    first_east = remote(part_ref.at[xo, lo], a_east, x_send.at[0], x_recv.at[0], east)
    first_west = remote(part_ref.at[xo, hi], a_west, x_send.at[1], x_recv.at[1], west)
    direct_east = remote(part_ref.at[xe, hi], d_hi, x_send.at[2], x_recv.at[2], east)
    direct_west = remote(part_ref.at[xw, lo], d_lo, x_send.at[3], x_recv.at[3], west)
    second_east = remote(s_east, b_lo, x_send.at[4], x_recv.at[4], east)
    second_west = remote(s_west, b_hi, x_send.at[5], x_recv.at[5], west)
    for copy in (first_east, first_west, direct_east, direct_west):
        copy.start()
    first_east.wait_recv()
    for b in range(HALF):
        s_east[b] = (a_east[b].astype(F32) + part_ref[xe, b].astype(F32)).astype(BF16)
    second_east.start()
    first_west.wait_recv()
    for b in range(HALF):
        s_west[b] = (a_west[b].astype(F32) + part_ref[xw, HALF + b].astype(F32)).astype(BF16)
    second_west.start()
    direct_east.wait_recv()
    direct_west.wait_recv()
    second_east.wait_recv()
    for b in range(HALF):
        total[b] = (part_ref[x, b].astype(F32) + d_lo[b].astype(F32) + b_lo[b].astype(F32)).astype(BF16)
    second_west.wait_recv()
    for b in range(HALF):
        total[HALF + b] = (
            part_ref[x, HALF + b].astype(F32) + d_hi[b].astype(F32) + b_hi[b].astype(F32)
        ).astype(BF16)

    def scatter_copy(k):
        return remote(total.at[lax.rem(b0 + k, RB)], landed.at[k], z_send.at[k], z_recv.at[k], peer(k))

    def scatter(k, carry):
        scatter_copy(k).start()
        return carry

    lax.fori_loop(1, RB, scatter, 0)

    def collect(k, running):
        scatter_copy(k).wait_recv()
        return running + landed[k].astype(F32)

    evolved = lax.fori_loop(1, RB, collect, total[b0].astype(F32))
    out_ref[x, b0] = (evolved * weight_ref[pl.ds(b0, 1), :]).astype(BF16)

    def gather_copy(k):
        return remote(out_ref.at[x, b0], out_ref.at[x, b0], a_send.at[k], a_recv.at[k], peer(k))

    def gather(k, carry):
        gather_copy(k).start()
        return carry

    def gathered(k, carry):
        slot = lax.rem(b0 + RB - k, RB)
        remote(out_ref.at[x, slot], out_ref.at[x, slot], a_send.at[k], a_recv.at[k], peer(k)).wait_recv()
        return carry

    lax.fori_loop(1, RB, gather, 0)
    lax.fori_loop(1, RB, gathered, 0)

    def along(q, part, n, device):
        return remote(out_ref.at[q, part], out_ref.at[q, part], g_send.at[n], g_recv.at[n], device)

    for copy in (along(x, lo, 0, east), along(x, hi, 1, west), along(x, hi, 2, east), along(x, lo, 3, west)):
        copy.start()
    along(xw, lo, 0, east).wait_recv()
    along(xw, lo, 4, east).start()
    along(xe, hi, 1, west).wait_recv()
    along(xe, hi, 5, west).start()
    along(xw, hi, 2, east).wait_recv()
    along(xe, lo, 3, west).wait_recv()
    along(xo, lo, 4, east).wait_recv()
    along(xo, hi, 5, west).wait_recv()

    def drain(k, carry):
        scatter_copy(k).wait_send()
        gather_copy(k).wait_send()
        return carry

    lax.fori_loop(1, RB, drain, 0)
    for copy in (first_east, first_west, direct_east, direct_west, second_east, second_west):
        copy.wait_send()
    along(x, lo, 0, east).wait_send()
    along(x, hi, 1, west).wait_send()
    along(x, hi, 2, east).wait_send()
    along(x, lo, 3, west).wait_send()
    along(xw, lo, 4, east).wait_send()
    along(xe, hi, 5, west).wait_send()


def combine_smooth(
    part_ref, kext_ref, probes_ref, out_ref,
    xl, xr, kb, fa, fb, adj, sib_far, sib_own, pre, relay, far, edge_out, edge_in,
    sf_send, sf_recv, so_send, so_recv, out_send, out_recv, rel_send, rel_recv, n_send, n_recv, s_send, s_recv,
):
    s, r, other, sib_r, far_sib_r, plus, minus, north, south = ring_places()
    sib = (s, sib_r)
    meet((north, south, sib, plus, minus))

    def sib_far_copy(g):
        return remote(part_ref.at[far_sib_r, :, g], sib_far.at[g], sf_send.at[g], sf_recv.at[g], sib)

    def sib_own_copy(g):
        return remote(part_ref.at[sib_r, :, g], sib_own.at[g], so_send.at[g], so_recv.at[g], sib)

    def outward_copy(g):
        return remote(pre.at[g], relay.at[g], out_send.at[g], out_recv.at[g], onward(g, plus, minus))

    def relay_copy(g):
        return remote(relay.at[g], far.at[g], rel_send.at[g], rel_recv.at[g], onward(g, plus, minus))

    def north_copy(g):
        return remote(edge_out.at[g, 0], edge_in.at[g, 1], n_send.at[g], n_recv.at[g], north)

    def south_copy(g):
        return remote(edge_out.at[g, 1], edge_in.at[g, 0], s_send.at[g], s_recv.at[g], south)

    def begin(g, carry):
        sib_far_copy(g).start()
        return carry

    lax.fori_loop(0, GROUPS, begin, 0)

    def begin_own(g, carry):
        sib_own_copy(g).start()
        return carry

    lax.fori_loop(0, GROUPS, begin_own, 0)

    def presum(g, carry):
        sib_far_copy(g).wait_recv()

        def block(j, inner):
            pre[g, j] = (part_ref[other, j, g].astype(F32) + sib_far[g, j].astype(F32)).astype(BF16)
            return inner

        lax.fori_loop(0, SB, block, 0, unroll=8)
        outward_copy(g).start()
        return carry

    lax.fori_loop(0, GROUPS, presum, 0)
    xl[...] = probes_ref[:, :BLK].astype(F32)
    xr[...] = probes_ref[:, BLK:].astype(F32)
    for l in range(PAD):
        kb[l] = jnp.broadcast_to(kext_ref[pl.ds(l + 4, 1), :], (GP, LON))
    lane = lax.broadcasted_iota(jnp.int32, (GP, LON), 1)

    def pass_on(g, carry):
        outward_copy(g).wait_recv()
        relay_copy(g).start()
        return carry

    lax.fori_loop(0, GROUPS, pass_on, 0)

    def finish_sum(g):
        sib_own_copy(g).wait_recv()
        relay_copy(g).wait_recv()
        for l in range(LAT):
            for h in range(2):
                j = 2 * l + h
                value = part_ref[r, j, g].astype(F32) + sib_own[g, j].astype(F32) + far[g, j].astype(F32)
                adj[g, l, :, h * BLK : (h + 1) * BLK] = value
                if l < STEPS:
                    edge_out[g, 0, l, :, h * BLK : (h + 1) * BLK] = value.astype(BF16)
                if l >= LAT - STEPS:
                    edge_out[g, 1, l - LAT + STEPS, :, h * BLK : (h + 1) * BLK] = value.astype(BF16)
        north_copy(g).start()
        south_copy(g).start()

    def smooth(g):
        north_copy(g).wait_recv()
        south_copy(g).wait_recv()
        for l in range(STEPS):
            fa[l] = edge_in[g, 0, l].astype(F32)
            fa[STEPS + LAT + l] = edge_in[g, 1, l].astype(F32)
        for l in range(LAT):
            fa[STEPS + l] = adj[g, l]
        base = pl.multiple_of(g * (GP * LAT), GP * LAT)
        for step in range(STEPS):
            for l in range(step, PAD - step):
                fb[l] = kb[l] * fa[l]
            for l in range(step + 1, PAD - step - 1):
                c = fb[l]
                v = fa[l] + (fb[l - 1] + fb[l + 1] + west_east(c, lane) - 4.0 * c)
                if step < STEPS - 1:
                    fa[l] = v
                else:
                    rows = pl.ds(base + l - STEPS, GP, stride=LAT)
                    xl[rows, :] = xl[rows, :] + v[:, :BLK]
                    xr[rows, :] = xr[rows, :] + v[:, BLK:]
        done = pl.ds(base, GP * LAT)
        out_ref[done, :BLK] = xl[done, :]
        out_ref[done, BLK:] = xr[done, :]

    def stage(g, carry):
        @pl.when(g < GROUPS)
        def _():
            finish_sum(g)

        @pl.when(g > 0)
        def _():
            smooth(g - 1)

        return carry

    lax.fori_loop(0, GROUPS + 1, stage, 0)

    def drain(g, carry):
        sib_far_copy(g).wait_send()
        sib_own_copy(g).wait_send()
        outward_copy(g).wait_send()
        relay_copy(g).wait_send()
        north_copy(g).wait_send()
        south_copy(g).wait_send()
        return carry

    lax.fori_loop(0, GROUPS, drain, 0)


def remote_params(n):
    return pltpu.CompilerParams(collective_id=n, has_side_effects=True)


def per_device(probes, kappa, footprint, block_source, block_receptor, block_count, obs_weight):
    flat = probes.reshape(PROBES * LAT, LON)
    blocks = footprint.reshape(NB, BLK, BLK)
    sources = block_source.reshape(NB)
    receptors = block_receptor.reshape(NB)
    count = block_count.reshape(1)
    pieces = (4, SB, GROUPS, GP, BLK)
    gathered, kext = pl.pallas_call(
        smooth_gather,
        out_shape=(jax.ShapeDtypeStruct(pieces, BF16), jax.ShapeDtypeStruct((32, LON), F32)),
        in_specs=[VM, VM],
        out_specs=(VM, VM),
        scratch_shapes=[
            pltpu.VMEM((PROBES * LAT, BLK), F32),
            pltpu.VMEM((PROBES * LAT, BLK), F32),
            pltpu.VMEM((PAD, PROBES, LON), BF16),
            pltpu.VMEM((PAD, GP, LON), F32),
            pltpu.VMEM((PAD, GP, LON), F32),
            pltpu.VMEM((PAD, GP, LON), F32),
            pltpu.VMEM((GROUPS, SB, GP, BLK), BF16),
        ]
        + [DMA((4,))] * 10,
        compiler_params=remote_params(0),
        name="smooth_gather",
    )(flat, kappa)
    part = pl.pallas_call(
        forward_blocks,
        out_shape=jax.ShapeDtypeStruct((4, RB, PROBES, BLK), BF16),
        in_specs=[SM, SM, SM, VM, ANY],
        out_specs=VM,
        scratch_shapes=[
            pltpu.VMEM((RB + 1, 4 * PROBES, BLK), F32),
            pltpu.VMEM((NB, BLK, BLK), BF16),
            DMA((NCHUNK,)),
        ],
        name="forward_blocks",
    )(sources, receptors, count, gathered.reshape(4, SB, PROBES, BLK), blocks)
    half = pltpu.VMEM((HALF, PROBES, BLK), BF16)
    whole = pltpu.VMEM((RB, PROBES, BLK), BF16)
    weighted = pl.pallas_call(
        reduce_weight_gather,
        out_shape=jax.ShapeDtypeStruct((4, RB, PROBES, BLK), BF16),
        in_specs=[VM, VM],
        out_specs=VM,
        scratch_shapes=[half] * 8
        + [whole] * 2
        + [DMA((6,)), DMA((6,)), DMA((RB,)), DMA((RB,)), DMA((RB,)), DMA((RB,)), DMA((6,)), DMA((6,))],
        compiler_params=remote_params(1),
        name="reduce_weight_gather",
    )(part, obs_weight.reshape(RB, BLK))
    terms = pl.pallas_call(
        adjoint_blocks,
        out_shape=jax.ShapeDtypeStruct((4, SB, PROBES, BLK), BF16),
        in_specs=[SM, SM, SM, VM, ANY],
        out_specs=VM,
        scratch_shapes=[
            pltpu.VMEM((SB + 1, 4 * PROBES, BLK), F32),
            pltpu.VMEM((NB, BLK, BLK), BF16),
            DMA((NCHUNK,)),
        ],
        name="adjoint_blocks",
    )(sources, receptors, count, weighted, blocks)
    slots = pltpu.VMEM((GROUPS, SB, GP, BLK), BF16)
    edges = pltpu.VMEM((GROUPS, 2, STEPS, GP, LON), BF16)
    rows = pltpu.VMEM((PAD, GP, LON), F32)
    result = pl.pallas_call(
        combine_smooth,
        out_shape=jax.ShapeDtypeStruct((PROBES * LAT, LON), F32),
        in_specs=[VM, VM, VM],
        out_specs=VM,
        scratch_shapes=[pltpu.VMEM((PROBES * LAT, BLK), F32)] * 2 + [rows, rows, rows, pltpu.VMEM((GROUPS, LAT, GP, LON), F32)]
        + [slots] * 5
        + [edges] * 2
        + [DMA((GROUPS,))] * 12,
        compiler_params=remote_params(2),
        name="combine_smooth",
    )(terms.reshape(pieces), kext, flat)
    return result.reshape(PROBES, LAT, LON)


def solution(mesh):
    placed = (
        P("rcv", "src", None),
        P("src", None),
        P("src", "rcv", None, None, None),
        P("src", "rcv", None),
        P("src", "rcv", None),
        P("src", "rcv"),
        P("rcv"),
    )
    return jax.shard_map(
        per_device, mesh=mesh, in_specs=placed, out_specs=P("rcv", "src", None), check_vma=False
    )
```
